512 devices in a mesh: dp: 256 (over z, y, x), ctx: 2 (over core).
Axes of the slice: x: 4, y: 8, z: 8, core: 2. Of those that a mesh axis runs over, the one named last changes fastest.
Arguments:
- head_inputs: bfloat16 [256, 512, 1024], P('dp', 'ctx'), may hold values from -6 to 6
- cotangent: bfloat16 [256, 512, 1024], P('dp', 'ctx'), may hold values from -6 to 6
- write_proj: bfloat16 [256, 512, 256], P('dp', 'ctx'), may hold values from -3 to 3
- read_proj: bfloat16 [256, 512, 256], P('dp', 'ctx'), may hold values from -3 to 3
- step_raw: float32 [256, 512, 16], P('dp', 'ctx'), may hold values from -4 to 4
- doc_index: int32 [256, 512], P('dp', 'ctx'), may hold values from 0 to 15, never falling along the last dimension, each value on 1 to 257 neighbouring positions
- log_rate: float32 [16], replicated, may hold values from 0 to 2.77
- step_bias: float32 [16], replicated, may hold values from -6.9 to -2.25
- skip_gain: float32 [16], replicated, may hold values from 0.5 to 1.5
Outputs:
- grad_inputs: bfloat16 [256, 512, 1024], P('dp', 'ctx')
- grad_write: bfloat16 [256, 512, 256], P('dp', 'ctx')
- grad_read: bfloat16 [256, 512, 256], P('dp', 'ctx')
- grad_step: float32 [256, 512, 16], P('dp', 'ctx')
- grad_rate: float32 [16], replicated
- grad_bias: float32 [16], replicated
- grad_skip: float32 [16], replicated
The draws below stay inside these ranges and needn't reach their ends.
Inputs may be any that keep to these rules, and one draw needn't show every extreme that they name: doc_index never falls along a sequence; each document spans 1 to 257 tokens and one of each sequence spans exactly that many.
All inputs are finite; a program needn't handle non-finite values.
Results may differ from the reference program's by a relative error of at most 0.0025.
Values may be sent and summed in bfloat16 or wider, within the bound.
No kernel may reach another device: no remote copies, remote signals or barrier semaphores. Data moves between devices by JAX's collectives and lax.ppermute only.
A program may use at most 64 MiB of HBM per device.

```python
import math
import jax
import jax.numpy as jnp
import numpy as np
from jax import lax

HEADS = 16
HEAD_DIM = 64
STATE = 256
BLOCK = 256
SEQS = 256
SEQ_LEN = 512


def block_levels(own_key, dims, cuts, smallest, high):
    level, own = 1.0, jax.random.fold_in(own_key, 6)
    for dim, shards_of in cuts:
        heights = jnp.exp(jax.random.uniform(jax.random.fold_in(own, dim), (shards_of,), jnp.float32, smallest / len(cuts), high / len(cuts)))
        level = level * jnp.repeat(heights, dims[dim] // shards_of).reshape([-1 if axis == dim else 1 for axis in range(len(dims))])
    return level


def length_profile(amount, total, reach, skew):
    loads = [(1 << 20) // math.isqrt(grade ** skew) + 1 for grade in range(2, amount + 1)]
    spare, counts = total - reach - (amount - 1), [1] * (amount - 1)
    while spare > 0:
        movable = [i for i in range(amount - 1) if counts[i] < reach]
        mass, remaining = sum([loads[i] for i in movable]), spare
        for i in movable:
            extra = min(reach - counts[i], max(1, remaining * loads[i] // mass), spare)
            counts[i] = counts[i] + extra
            spare = spare - extra
    return np.array([reach] + counts)


def uneven_parts(key, count, total, reach, slope):
    if count == 2:
        one = jax.random.randint(key, (), max(1, total - reach), min(reach, total - 1) + 1)
        return jnp.stack([one, total - one])
    sizes = jnp.asarray(length_profile(count, total, reach, slope), jnp.int32)
    twos = (count - 1) // 2
    donor, sink = sizes[1:1 + 2 * twos:2], sizes[2:2 + 2 * twos:2]
    margin = jnp.minimum(donor - 1, reach - sink)
    shifted = jax.random.randint(jax.random.fold_in(key, 1), (twos,), 0, 1 << 20) % (margin + 1)
    sizes = sizes.at[1:1 + 2 * twos:2].set(donor - shifted).at[2:2 + 2 * twos:2].set(sink + shifted)
    return sizes[jax.random.permutation(jax.random.fold_in(key, 2), count)]


def noise(own_key, shape, scale, reach, shards=(), dtype=jnp.bfloat16):
    drawn = jax.random.normal(own_key, shape, jnp.float32) * scale
    if len(shards) > 0:
        drawn = block_levels(own_key, shape, shards, -0.22, 0.18) * drawn
    return jnp.clip(drawn, min=-reach, max=reach).astype(dtype)


def setup_inputs(seed: int = 0) -> dict:
    keys = jax.random.split(jax.random.key(seed), 10)
    return {
        "head_inputs": noise(keys[0], (SEQS, SEQ_LEN, HEADS * HEAD_DIM), 1.0, 6.0, ((0, 256), (1, 2))),
        "cotangent": noise(keys[1], (SEQS, SEQ_LEN, HEADS * HEAD_DIM), 1.0, 6.0, ((0, 256), (1, 2))),
        "write_proj": noise(keys[2], (SEQS, SEQ_LEN, STATE), 0.5, 3.0, ((0, 256), (1, 2))),
        "read_proj": noise(keys[3], (SEQS, SEQ_LEN, STATE), 0.5, 3.0, ((0, 256), (1, 2))),
        "step_raw": noise(keys[4], (SEQS, SEQ_LEN, HEADS), 1.0, 4.0, ((0, 256), (1, 2)), jnp.float32),
        "doc_index": jax.vmap(lambda own: jnp.searchsorted(jnp.cumsum(uneven_parts(own, 16, SEQ_LEN, SEQ_LEN // 2 + 1, 2)), jnp.arange(SEQ_LEN), side="right"))(jax.random.split(keys[5], SEQS)).reshape((SEQS, SEQ_LEN)).astype(jnp.int32),
        "log_rate": jnp.clip(jax.random.uniform(keys[6], (HEADS,), jnp.float32, 0.0, 2.77), 0.0, 2.77),
        "step_bias": jnp.clip(jax.random.uniform(keys[7], (HEADS,), jnp.float32, -6.9, -2.25), -6.9, -2.25),
        "skip_gain": jnp.clip(jax.random.uniform(keys[8], (HEADS,), jnp.float32, 0.5, 1.5), 0.5, 1.5),
    }


def ssd_forward(inputs, writes, reads, steps, segment, segment_prev, state_init, log_rate, skip_gain):
    length, heads, width = inputs.shape
    count = length // BLOCK
    rate_all = steps * (-jnp.exp(log_rate))[None, :]
    blocks = (inputs.reshape(count, BLOCK, heads, width), writes.reshape(count, BLOCK, -1), reads.reshape(count, BLOCK, -1), steps.reshape(count, BLOCK, heads), rate_all.reshape(count, BLOCK, heads), segment.reshape(count, BLOCK))
    causal = jnp.arange(BLOCK)[:, None] >= jnp.arange(BLOCK)[None, :]
    highest = lax.Precision.HIGHEST

    def advance(carry, piece):
        state, last_doc = carry
        in_block, write_block, read_block, step_block, rate_block, doc_block = piece
        cumulative = jnp.cumsum(rate_block, axis=0)
        same_doc = causal & (doc_block[:, None] == doc_block[None, :])
        gaps = cumulative[:, None, :] - cumulative[None, :, :]
        decay = jnp.exp(jnp.where(same_doc[:, :, None], gaps, -1e+30))
        scores = jnp.einsum('in,jn->ij', read_block, write_block, precision=highest)
        mixing = decay * (scores[:, :, None] * step_block[None, :, :])
        result = jnp.einsum('ijh,jhp->ihp', mixing, in_block, precision=highest)
        keep = (doc_block == last_doc).astype(jnp.float32)
        start = jnp.exp(cumulative) * keep[:, None]
        result = result + jnp.einsum('in,hpn->ihp', read_block, state, precision=highest) * start[:, :, None]
        result = result + skip_gain[None, :, None] * in_block
        end_doc = doc_block[BLOCK - 1]
        tail = jnp.exp(cumulative[BLOCK - 1][None, :] - cumulative) * (doc_block == end_doc).astype(jnp.float32)[:, None] * step_block
        carried = jnp.exp(cumulative[BLOCK - 1]) * (end_doc == last_doc).astype(jnp.float32)
        state = carried[:, None, None] * state + jnp.einsum('jh,jhp,jn->hpn', tail, in_block, write_block, precision=highest)
        return ((state, end_doc), result)
    (state, _), results = lax.scan(jax.checkpoint(advance), (state_init, segment_prev), blocks)
    return (results.reshape(length, heads, width), state)

def layer_grads(inputs, cotangent, writes, reads, step_raw, segment, segment_prev, state_init, log_rate, step_bias, skip_gain, state_grad):
    length = inputs.shape[0]
    heads = step_raw.shape[1]
    head_view = inputs.astype(jnp.float32).reshape(length, heads, HEAD_DIM)

    def forward(head_view, writes, reads, step_raw, log_rate, step_bias, skip_gain):
        steps = jax.nn.softplus(step_raw + step_bias[None, :])
        return ssd_forward(head_view, writes, reads, steps, segment, segment_prev, state_init, log_rate, skip_gain)
    _, pullback = jax.vjp(forward, head_view, writes.astype(jnp.float32), reads.astype(jnp.float32), step_raw, log_rate, step_bias, skip_gain)
    return pullback((cotangent.astype(jnp.float32).reshape(length, heads, HEAD_DIM), state_grad))

def reference(head_inputs, cotangent, write_proj, read_proj, step_raw, doc_index, log_rate, step_bias, skip_gain):

    def per_sequence(items):
        inputs, cotan_rows, writes, reads, raw_steps, segment = items
        zero_state = jnp.zeros((HEADS, HEAD_DIM, STATE), jnp.float32)
        grads = layer_grads(inputs, cotan_rows, writes, reads, raw_steps, segment, segment[0], zero_state, log_rate, step_bias, skip_gain, zero_state)
        return (grads[0].reshape(inputs.shape[0], -1).astype(jnp.bfloat16), grads[1].astype(jnp.bfloat16), grads[2].astype(jnp.bfloat16), grads[3], grads[4], grads[5], grads[6])
    results = lax.map(per_sequence, (head_inputs, cotangent, write_proj, read_proj, step_raw, doc_index))
    return (results[0], results[1], results[2], results[3], lax.optimization_barrier(jnp.sum(results[4], axis=0)), lax.optimization_barrier(jnp.sum(results[5], axis=0)), lax.optimization_barrier(jnp.sum(results[6], axis=0)))
```

```python
import jax
import jax.numpy as jnp
from jax import lax
from jax.experimental import pallas as pl
from jax.experimental.pallas import tpu as pltpu
from jax.sharding import PartitionSpec as P

HEADS = 16
HEAD_DIM = 64
STATE = 256
BLOCK = 256
WIDTH = HEADS * HEAD_DIM
HALF = BLOCK // 2
PAIR = 2 * HEAD_DIM
F32 = jnp.float32
BF16 = jnp.bfloat16
NEG = -1e30

NN = (((1,), (0,)), ((), ()))
NT = (((1,), (1,)), ((), ()))


def dot(a, b, dims=NN):
    return lax.dot_general(a, b, dims, preferred_element_type=F32)


def split2(v):
    hi = v.astype(BF16)
    return hi, (v - hi.astype(F32)).astype(BF16)


def split3(v):
    hi = v.astype(BF16)
    rest = v - hi.astype(F32)
    mid = rest.astype(BF16)
    return hi, mid, (rest - mid.astype(F32)).astype(BF16)


def softplus(z):
    u = jnp.exp(-jnp.abs(z))
    series = u * (1.0 - u * (0.5 - u * (1.0 / 3.0 - u * 0.25)))
    return jnp.maximum(z, 0.0) + jnp.where(u < 0.01, series, jnp.log(1.0 + u))


def head_rows():
    lane = lax.broadcasted_iota(jnp.int32, (HEADS, WIDTH), 1)
    head = lax.broadcasted_iota(jnp.int32, (HEADS, WIDTH), 0)
    return (lax.shift_right_logical(lane, 6) == head).astype(BF16)


def expand(v, rows):
    hi, mid, lo = split3(v)
    return dot(hi, rows) + dot(mid, rows) + dot(lo, rows)


def head_sums(v, rows):
    hi, mid, lo = split3(v)
    return dot(hi, rows, NT) + dot(mid, rows, NT) + dot(lo, rows, NT)


def tri_ones(lower):
    r = lax.broadcasted_iota(jnp.int32, (BLOCK, BLOCK), 0)
    c = lax.broadcasted_iota(jnp.int32, (BLOCK, BLOCK), 1)
    return ((r >= c) if lower else (r <= c)).astype(BF16)


def transpose_heads(v):
    wide = jnp.concatenate([v, jnp.zeros((BLOCK, 128 - HEADS), F32)], axis=1)
    return wide.T[0:HEADS]


def columns(row):
    return jnp.broadcast_to(row, (128, BLOCK)).T


def outgoing_kernel(
    doc_ref, raw_ref, bias_ref, lr_ref, x_ref, c_ref, w_ref, r_ref,
    send_ref, f_ref, s_ref, cum_ref, cumt_ref,
):
    first = lax.axis_index("ctx") == 0
    z = raw_ref[0] + bias_ref[...]
    s = softplus(z)
    rate = s * (-jnp.exp(lr_ref[...]))
    tri = tri_ones(True)
    hi, mid, lo = split3(rate)
    cum = dot(tri, hi) + dot(tri, mid) + dot(tri, lo)
    s_ref[...] = s
    cum_ref[...] = cum
    cumt_ref[...] = transpose_heads(cum)
    doc = doc_ref[...].astype(F32)
    doc_col = columns(doc)[:, 0:HEADS]
    edge = jnp.where(first, doc[:, BLOCK - 1 :], doc[:, 0:1])
    arg = jnp.where(first, cum[BLOCK - 1 :] - cum, cum)
    gain = jnp.where(first, s, jnp.ones_like(s))
    f = jnp.where(doc_col == edge, jnp.exp(arg) * gain, 0.0)
    f_ref[...] = f
    wide = expand(f, head_rows())
    v = jnp.where(first, x_ref[0], c_ref[0]).astype(F32) * wide
    k = jnp.where(first, w_ref[0], r_ref[0]).T
    hi, lo = split2(v)
    send_ref[0:STATE] = dot(k, hi) + dot(k, lo)
    send_ref[STATE:] = jnp.broadcast_to(edge, (8, WIDTH))


def intra_kernel(
    doc_ref, s_ref, cum_ref, cumt_ref, x_ref, c_ref, w_ref, r_ref,
    dx_ref, dw_ref, dr_ref, col_ref,
    mask_ref, p_ref, dp_ref, colt_ref,
):
    doc = doc_ref[...].astype(F32)
    doc_col = columns(doc)
    for t in range(2):
        span = slice(t * HALF, (t + 1) * HALF)
        j = lax.broadcasted_iota(jnp.int32, (BLOCK, HALF), 0)
        i = lax.broadcasted_iota(jnp.int32, (BLOCK, HALF), 1) + t * HALF
        ok = (i >= j) & (doc_col == doc[:, span])
        mask_ref[:, span] = jnp.where(ok, 0.0, NEG)
    p_ref[...] = dot(w_ref[0], r_ref[0], NT)
    dp_ref[...] = jnp.zeros((BLOCK, BLOCK), F32)
    colj = cum_ref[...] - jnp.log(s_ref[...])
    lane = lax.broadcasted_iota(jnp.int32, (BLOCK, PAIR), 1)
    for pair in range(HEADS // 2):
        lanes = slice(pair * PAIR, (pair + 1) * PAIR)
        xp, cp = x_ref[0, :, lanes], c_ref[0, :, lanes]
        top = bottom = None
        for odd in range(2):
            h = 2 * pair + odd
            ch = jnp.where((lane < HEAD_DIM) != bool(odd), cp, jnp.zeros_like(cp))
            row = cumt_ref[h : h + 1, :]
            col = colj[:, h : h + 1]

            def tile(js, isl):
                g = dot(xp[js], ch[isl], NT)
                ell = jnp.exp((row[:, isl] - col[js]) + mask_ref[js, isl])
                m = ell * p_ref[js, isl]
                dp_ref[js, isl] += ell * g
                hi, lo = split2(m)
                return dot(hi, ch[isl]) + dot(lo, ch[isl]), jnp.sum(m * g, axis=0, keepdims=True)

            d0, e0 = tile(slice(0, HALF), slice(0, BLOCK))
            d1, e1 = tile(slice(HALF, BLOCK), slice(HALF, BLOCK))
            colt_ref[h : h + 1, 0:HALF] = e0[:, 0:HALF]
            colt_ref[h : h + 1, HALF:] = e0[:, HALF:] + e1
            top = d0 if top is None else top + d0
            bottom = d1 if bottom is None else bottom + d1
        dx_ref[0:HALF, lanes] = top
        dx_ref[HALF:, lanes] = bottom
    dp = dp_ref[...]
    hi, lo = split2(dp)
    dw_ref[...] = dot(hi, r_ref[0]) + dot(lo, r_ref[0])
    hi, lo = split2(dp.T)
    dr_ref[...] = dot(hi, w_ref[0]) + dot(lo, w_ref[0])
    col_ref[...] = colt_ref[...].T[:, 0:HEADS]


def final_kernel(
    got_ref, doc_ref, raw_ref, bias_ref, lr_ref, skip_ref, f_ref, s_ref,
    x_ref, c_ref, w_ref, r_ref, dxi_ref, dwi_ref, dri_ref, col_ref,
    dx_ref, dw_ref, dr_ref, dstep_ref, sums_ref,
):
    first = lax.axis_index("ctx") == 0
    doc = doc_ref[...].astype(F32)
    edge = jnp.where(first, doc[:, BLOCK - 1 :], doc[:, 0:1])
    joined = (got_ref[STATE : STATE + 1, 0:1] == edge).astype(F32)
    rows = head_rows()
    f = f_ref[...] * joined
    s = s_ref[...]
    wide = expand(f, rows)
    x, c = x_ref[0].astype(F32), c_ref[0].astype(F32)
    v = jnp.where(first, x, c)
    k = jnp.where(first, w_ref[0], r_ref[0])
    t_hi, t_lo = split2(got_ref[0:STATE])
    zs = (dot(k, t_hi) + dot(k, t_lo)) * wide
    vf_hi, vf_lo = split2(v * wide)
    dk = dot(vf_hi, t_hi, NT) + dot(vf_lo, t_hi, NT) + dot(vf_hi, t_lo, NT)
    zero = jnp.zeros_like(dk)
    dw_ref[0] = (dwi_ref[...] + jnp.where(first, dk, zero)).astype(BF16)
    dr_ref[0] = (dri_ref[...] + jnp.where(first, zero, dk)).astype(BF16)
    u = head_sums(v * zs, rows)
    dxi = dxi_ref[...]
    q = head_sums(x * dxi, rows)
    gains = expand(jnp.broadcast_to(skip_ref[...], (8, HEADS)), rows)[0:1]
    dx = dxi + jnp.where(first, zs, 0.0) + gains * c
    dx_ref[0] = dx.astype(BF16)
    q = q + jnp.where(first, u, 0.0)
    da = col_ref[...] - q + jnp.where(first, 0.0, u)
    hi, mid, lo = split3(da)
    tri = tri_ones(False)
    drate = dot(tri, hi) + dot(tri, mid) + dot(tri, lo)
    drate = drate + jnp.where(first, jnp.sum(u, axis=0, keepdims=True), 0.0)
    ell = jnp.exp(lr_ref[...])
    z = raw_ref[0] + bias_ref[...]
    dstep = (q / s - drate * ell) / (1.0 + jnp.exp(-z))
    dstep_ref[0] = dstep
    sum_bias = jnp.sum(dstep, axis=0, keepdims=True)
    sum_rate = jnp.sum(drate * (s * -ell), axis=0, keepdims=True)
    cx = jnp.sum(c * x, axis=0, keepdims=True)
    sum_skip = head_sums(jnp.broadcast_to(cx, (8, WIDTH)), rows)[0:1]
    pad = jnp.zeros((1, 128 - 3 * HEADS), F32)
    sums_ref[...] = jnp.concatenate([sum_rate, sum_bias, sum_skip, pad], axis=1)


def call(kernel, outs, scratch=(), flops=0, bytes_accessed=0):
    return pl.pallas_call(
        kernel,
        out_shape=outs,
        scratch_shapes=list(scratch),
        compiler_params=pltpu.CompilerParams(vmem_limit_bytes=40 << 20),
        cost_estimate=pl.CostEstimate(
            flops=flops, bytes_accessed=bytes_accessed, transcendentals=0
        ),
    )


def shape(dims, dtype=F32):
    return jax.ShapeDtypeStruct(dims, dtype)


def mesh_sum(sums, devices):
    sums = lax.psum(sums, "ctx")
    everyone = jnp.broadcast_to(sums, (devices, 128))
    everyone = lax.all_to_all(everyone, "dp", split_axis=0, concat_axis=0, tiled=True)
    return jnp.sum(everyone, axis=0)


def on_device(x, c, w, r, raw, doc, log_rate, step_bias, skip_gain):
    lr, bias, skip = log_rate[None], step_bias[None], skip_gain[None]
    per_head = shape((BLOCK, HEADS))
    send, f, s, cum, cumt = call(
        outgoing_kernel,
        (shape((STATE + 8, WIDTH)), per_head, per_head, per_head, shape((HEADS, BLOCK))),
        flops=300_000_000,
        bytes_accessed=3 << 20,
    )(doc, raw, bias, lr, x, c, w, r)
    got = lax.ppermute(send, "ctx", [(0, 1), (1, 0)])
    square = shape((BLOCK, STATE))
    dxi, dwi, dri, col = call(
        intra_kernel,
        (shape((BLOCK, WIDTH)), square, square, per_head),
        scratch=(
            pltpu.VMEM((BLOCK, BLOCK), F32),
            pltpu.VMEM((BLOCK, BLOCK), F32),
            pltpu.VMEM((BLOCK, BLOCK), F32),
            pltpu.VMEM((HEADS, BLOCK), F32),
        ),
        flops=2_000_000_000,
        bytes_accessed=4 << 20,
    )(doc, s, cum, cumt, x, c, w, r)
    grad_x, grad_w, grad_r, grad_step, sums = call(
        final_kernel,
        (
            shape((1, BLOCK, WIDTH), BF16),
            shape((1, BLOCK, STATE), BF16),
            shape((1, BLOCK, STATE), BF16),
            shape((1, BLOCK, HEADS)),
            shape((1, 128)),
        ),
        flops=1_000_000_000,
        bytes_accessed=5 << 20,
    )(got, doc, raw, bias, lr, skip, f, s, x, c, w, r, dxi, dwi, dri, col)
    total = mesh_sum(sums, lax.axis_size("dp"))
    return (
        grad_x, grad_w, grad_r, grad_step,
        total[0:HEADS], total[HEADS : 2 * HEADS], total[2 * HEADS : 3 * HEADS],
    )


def solution(mesh):
    split = P("dp", "ctx", None)
    return jax.shard_map(
        on_device,
        mesh=mesh,
        in_specs=(split, split, split, split, split, P("dp", "ctx"), P(), P(), P()),
        out_specs=(split, split, split, split, P(), P(), P()),
        check_vma=False,
    )
```

```python
import jax
import jax.numpy as jnp
from jax import lax
from jax.experimental import pallas as pl
from jax.experimental.pallas import tpu as pltpu
from jax.sharding import PartitionSpec as P

HEADS = 16
HEAD_DIM = 64
STATE = 256
BLOCK = 256
WIDTH = HEADS * HEAD_DIM
HALF = BLOCK // 2
PAIR = 2 * HEAD_DIM
F32 = jnp.float32
BF16 = jnp.bfloat16
NEG = -1e30
LOG2E = 1.4426950408889634
LEFT = 1500

NN = (((1,), (0,)), ((), ()))
NT = (((1,), (1,)), ((), ()))


def dot(a, b, dims=NN):
    return lax.dot_general(a, b, dims, preferred_element_type=F32)


def split2(v):
    hi = v.astype(BF16)
    return hi, (v - hi.astype(F32)).astype(BF16)


def split3(v):
    hi = v.astype(BF16)
    rest = v - hi.astype(F32)
    mid = rest.astype(BF16)
    return hi, mid, (rest - mid.astype(F32)).astype(BF16)


def softplus(z):
    u = jnp.exp(-jnp.abs(z))
    series = u * (1.0 - u * (0.5 - u * (1.0 / 3.0 - u * 0.25)))
    return jnp.maximum(z, 0.0) + jnp.where(u < 0.01, series, jnp.log(1.0 + u))


def head_rows(count, start=0, width=WIDTH):
    lane = lax.broadcasted_iota(jnp.int32, (count, width), 1) + start
    row = lax.broadcasted_iota(jnp.int32, (count, width), 0)
    hit = lax.shift_right_logical(lane, 6) == (row & (HEADS - 1))
    return (hit & (row < 3 * HEADS)).astype(BF16)


def pieces(v):
    parts = [part.astype(F32) for part in split3(v)]
    rest = jnp.zeros((128 - 3 * HEADS, BLOCK), F32)
    return jnp.concatenate(parts + [rest], axis=0).T.astype(BF16)


def head_sums(v, rows):
    hi, lo = split2(v)
    return dot(rows, hi, NT) + dot(rows, lo, NT)


def triangle(upper):
    r = lax.broadcasted_iota(jnp.int32, (BLOCK, BLOCK), 0)
    c = lax.broadcasted_iota(jnp.int32, (BLOCK, BLOCK), 1)
    return ((r <= c) if upper else (r >= c)).astype(BF16)


def along_tokens(v, tri):
    count = v.shape[0]
    sums = dot(jnp.concatenate(split3(v), axis=0), tri)
    return sums[0:count] + sums[count : 2 * count] + sums[2 * count :]


def columns(row):
    return jnp.broadcast_to(row, (128, BLOCK)).T


def eye():
    r = lax.broadcasted_iota(jnp.int32, (HEADS, HEADS), 0)
    c = lax.broadcasted_iota(jnp.int32, (HEADS, HEADS), 1)
    return r == c


def to_column(row):
    return jnp.sum(jnp.where(eye(), row, 0.0), axis=1, keepdims=True)


def to_row(column):
    return jnp.sum(jnp.where(eye(), column, 0.0), axis=0, keepdims=True)


def head_arrays(raw, bias, lr):
    ell = jnp.exp(to_column(lr))
    z = raw + to_column(bias)
    s = softplus(z)
    return z, s, ell, s * -ell


def edge_gain(first, doc, s, cum):
    edge = jnp.where(first, doc[:, BLOCK - 1 :], doc[:, 0:1])
    arg = jnp.where(first, cum[:, BLOCK - 1 :] - cum, cum)
    gain = jnp.where(first, s, jnp.ones_like(s))
    return edge, jnp.where(doc == edge, jnp.exp(arg) * gain, 0.0)


PARTS = 4
PART = WIDTH // PARTS


def outgoing_kernel(
    doc_hbm, raw_hbm, bias_hbm, lr_hbm, x_hbm, c_hbm, w_hbm, r_hbm,
    send_hbm,
    doc_ref, raw_ref, bias_ref, lr_ref, v_ref, k_ref, send_ref, sems, out_sems,
):
    core = lax.axis_index("ctx")
    first = core == 0
    small = [
        pltpu.make_async_copy(src, dst, sems.at[n])
        for n, (src, dst) in enumerate(
            ((raw_hbm, raw_ref), (bias_hbm, bias_ref), (lr_hbm, lr_ref), (doc_hbm, doc_ref))
        )
    ]
    for copy in small:
        copy.start()

    def fetch_k(src):
        return pltpu.make_async_copy(src.at[0], k_ref, sems.at[4])

    def fetch_v(src, n):
        lanes = slice(n * PART, (n + 1) * PART)
        return pltpu.make_async_copy(src.at[0, :, lanes], v_ref.at[:, lanes], sems.at[5 + n])

    sources = ((w_hbm, x_hbm), (r_hbm, c_hbm))
    for which in range(2):

        @pl.when(core == which)
        def _():
            fetch_k(sources[which][0]).start()
            for n in range(PARTS):
                fetch_v(sources[which][1], n).start()

    tri = triangle(True)
    for copy in small:
        copy.wait()
    doc = doc_ref[...].astype(F32)
    _, s, _, rate = head_arrays(raw_ref[0], bias_ref[...], lr_ref[...])
    edge, f = edge_gain(first, doc, s, along_tokens(rate, tri))
    by_token = pieces(f)
    send_ref[STATE:] = jnp.broadcast_to(edge, (8, WIDTH))
    out = [pltpu.make_async_copy(send_ref.at[STATE:], send_hbm.at[STATE:], out_sems.at[PARTS])]
    out[0].start()
    fetch_k(w_hbm).wait()
    k = k_ref[...].T
    for n in range(PARTS):
        lanes = slice(n * PART, (n + 1) * PART)
        wide = dot(by_token, head_rows(128, n * PART, PART))
        fetch_v(x_hbm, n).wait()
        hi, lo = split2(v_ref[:, lanes].astype(F32) * wide)
        send_ref[0:STATE, lanes] = dot(k, hi) + dot(k, lo)
        copy = pltpu.make_async_copy(
            send_ref.at[0:STATE, lanes], send_hbm.at[0:STATE, lanes], out_sems.at[n]
        )
        copy.start()
        out.append(copy)
    for copy in out:
        copy.wait()


STEP, GAIN, SIG, ELL, COL, ROW = (HEADS * n for n in range(6))
KEPT = ROW + HEADS
W_RATE, W_BIAS, OWN, EDGE = 0, HEADS, 2 * HEADS, 2 * HEADS + 8


def intra_kernel(
    doc_ref, raw_ref, bias_ref, lr_ref, x_ref, c_ref, w_ref, r_ref,
    dx_ref, dp_ref, heads_ref, aux_ref,
    mask_ref, p_ref,
):
    first = lax.axis_index("ctx") == 0
    doc = doc_ref[...].astype(F32)
    z, s, ell, rate = head_arrays(raw_ref[0], bias_ref[...], lr_ref[...])
    sig = 1.0 / (1.0 + jnp.exp(-z))
    both = along_tokens(jnp.concatenate([rate, sig], axis=0), triangle(True))
    cum, cum_sig = both[0:HEADS], both[HEADS:]
    edge, f = edge_gain(first, doc, s, cum)
    heads_ref[STEP:GAIN] = s
    heads_ref[GAIN:SIG] = f
    heads_ref[SIG:ELL] = sig
    heads_ref[ELL:COL] = jnp.broadcast_to(ell, (HEADS, BLOCK))
    doc_col = columns(doc)
    for t in range(2):
        span = slice(t * HALF, (t + 1) * HALF)
        j = lax.broadcasted_iota(jnp.int32, (BLOCK, HALF), 0)
        i = lax.broadcasted_iota(jnp.int32, (BLOCK, HALF), 1) + t * HALF
        ok = (i >= j) & (doc_col == doc[:, span])
        mask_ref[:, span] = jnp.where(ok, 0.0, NEG)
    p_ref[...] = dot(w_ref[0], r_ref[0], NT)
    dp_ref[...] = jnp.zeros((BLOCK, BLOCK), F32)
    rows2 = cum * LOG2E
    cols2 = jnp.concatenate([(cum - jnp.log(s)) * LOG2E, jnp.zeros((128 - HEADS, BLOCK), F32)], axis=0).T
    lane = lax.broadcasted_iota(jnp.int32, (BLOCK, PAIR), 1)
    for pair in range(HEADS // 2):
        lanes = slice(pair * PAIR, (pair + 1) * PAIR)
        xp, cp = x_ref[0, :, lanes], c_ref[0, :, lanes]
        top = bottom = None
        for odd in range(2):
            h = 2 * pair + odd
            ch = jnp.where((lane < HEAD_DIM) != bool(odd), cp, jnp.zeros_like(cp))
            row = rows2[h : h + 1, :]
            col = cols2[:, h : h + 1]

            def tile(js, isl):
                g = dot(xp[js], ch[isl], NT)
                decay = jnp.exp2((row[:, isl] - col[js]) + mask_ref[js, isl])
                m = decay * p_ref[js, isl]
                dp_ref[js, isl] += decay * g
                hi, lo = split2(m)
                return dot(hi, ch[isl]) + dot(lo, ch[isl]), jnp.sum(m * g, axis=0, keepdims=True)

            d0, e0 = tile(slice(0, HALF), slice(0, BLOCK))
            d1, e1 = tile(slice(HALF, BLOCK), slice(HALF, BLOCK))
            heads_ref[ROW + h : ROW + h + 1, 0:HALF] = e0[:, 0:HALF]
            heads_ref[ROW + h : ROW + h + 1, HALF:] = e0[:, HALF:] + e1
            top = d0 if top is None else top + d0
            bottom = d1 if bottom is None else bottom + d1
        dx_ref[0:HALF, lanes] = top
        dx_ref[HALF:, lanes] = bottom
    rows = head_rows(HEADS)
    x = x_ref[0].astype(F32)
    q = head_sums(x * dx_ref[...], rows)
    heads_ref[COL:ROW] = q
    cx = jnp.sum(c_ref[0].astype(F32) * x, axis=0, keepdims=True)
    skip = sum(dot(rows, part, NT) for part in split3(jnp.broadcast_to(cx, (128, WIDTH))))
    da = heads_ref[ROW:] - q
    over = sig / s
    own_rate = jnp.sum(da * cum, axis=1, keepdims=True)
    own_bias = jnp.sum(q * over - ell * (da * cum_sig), axis=1, keepdims=True)
    own = [to_row(own_rate), to_row(own_bias), to_row(skip[:, 0:1])]
    own = jnp.concatenate(own + [jnp.zeros((1, BLOCK - 3 * HEADS), F32)], axis=1)
    w_rate = jnp.where(first, cum[:, BLOCK - 1 :] - cum, cum)
    w_bias = jnp.where(first, over + ell * (cum_sig - cum_sig[:, BLOCK - 1 :]), -ell * cum_sig)
    aux_ref[W_RATE:W_BIAS] = f * w_rate
    aux_ref[W_BIAS:OWN] = f * w_bias
    aux_ref[OWN:EDGE] = jnp.broadcast_to(own, (8, BLOCK))
    aux_ref[EDGE:] = jnp.broadcast_to(edge, (8, BLOCK))


def joined(got_ref, aux_ref):
    return (got_ref[STATE : STATE + 1, 0:1] == aux_ref[EDGE : EDGE + 1, 0:1]).astype(F32)


def sums_kernel(got_ref, aux_ref, x_ref, c_ref, w_ref, r_ref, sums_ref):
    first = lax.axis_index("ctx") == 0
    v = jnp.where(first, x_ref[0], c_ref[0]).astype(F32)
    k = jnp.where(first, w_ref[0], r_ref[0])
    t_hi, t_lo = split2(got_ref[0:STATE])
    z = dot(k, t_hi) + dot(k, t_lo)
    u = head_sums(v * z, head_rows(HEADS)) * joined(got_ref, aux_ref)
    sum_rate = to_row(jnp.sum(u * aux_ref[W_RATE:W_BIAS], axis=1, keepdims=True))
    sum_bias = to_row(jnp.sum(u * aux_ref[W_BIAS:OWN], axis=1, keepdims=True))
    rest = jnp.zeros((1, 128 - 2 * HEADS), F32)
    cross = jnp.concatenate([sum_rate, sum_bias, rest], axis=1)
    sums_ref[...] = aux_ref[OWN : OWN + 1, 0:128] + cross


def grads_kernel(
    got_ref, aux_ref, heads_ref, skip_ref, x_ref, c_ref, w_ref, r_ref, dxi_ref, dp_ref,
    dx_ref, dw_ref, dr_ref, dstep_ref,
):
    first = lax.axis_index("ctx") == 0
    f = heads_ref[GAIN:SIG] * joined(got_ref, aux_ref)
    wide = dot(pieces(f), head_rows(128))
    c = c_ref[0].astype(F32)
    v = jnp.where(first, x_ref[0], c_ref[0]).astype(F32)
    k = jnp.where(first, w_ref[0], r_ref[0])
    t_hi, t_lo = split2(got_ref[0:STATE])
    zs = (dot(k, t_hi) + dot(k, t_lo)) * wide
    hi, lo = split2(v * wide)
    dk = dot(hi, t_hi, NT) + dot(lo, t_hi, NT) + dot(hi, t_lo, NT)
    zero = jnp.zeros_like(dk)
    hi, lo = split2(dp_ref[...])
    dw = dot(hi, r_ref[0]) + dot(lo, r_ref[0])
    hi, lo = split2(dp_ref[...].T)
    dr = dot(hi, w_ref[0]) + dot(lo, w_ref[0])
    dw_ref[0] = (dw + jnp.where(first, dk, zero)).astype(BF16)
    dr_ref[0] = (dr + jnp.where(first, zero, dk)).astype(BF16)
    gains = dot(pieces(jnp.broadcast_to(to_column(skip_ref[...]), (HEADS, BLOCK))), head_rows(128))
    dx = dxi_ref[...] + jnp.where(first, zs, 0.0) + gains * c
    dx_ref[0] = dx.astype(BF16)
    u = head_sums(v * zs, head_rows(HEADS))
    q = heads_ref[COL:ROW] + jnp.where(first, u, 0.0)
    da = heads_ref[ROW:] - q + jnp.where(first, 0.0, u)
    drate = along_tokens(da, triangle(False))
    drate = drate + jnp.where(first, jnp.sum(u, axis=1, keepdims=True), 0.0)
    dstep = (q / heads_ref[STEP:GAIN] - drate * heads_ref[ELL:COL]) * heads_ref[SIG:ELL]
    dstep_ref[0] = dstep


def call(kernel, outs, scratch=(), limit=40 << 10, flops=0, bytes_accessed=0, **specs):
    return pl.pallas_call(
        kernel,
        out_shape=outs,
        scratch_shapes=list(scratch),
        compiler_params=pltpu.CompilerParams(vmem_limit_bytes=limit << 10),
        cost_estimate=pl.CostEstimate(
            flops=flops, bytes_accessed=bytes_accessed, transcendentals=0
        ),
        **specs,
    )


def shape(dims, dtype=F32):
    return jax.ShapeDtypeStruct(dims, dtype)


def mesh_sum(sums, devices):
    both = lax.all_gather(sums, "ctx", axis=0, tiled=True)
    sums = both[0:1] + both[1:2]
    everyone = jnp.broadcast_to(sums, (devices, 128))
    everyone = lax.all_to_all(everyone, "dp", split_axis=0, concat_axis=0, tiled=True)
    return jnp.sum(everyone, axis=0)


def on_device(x, c, w, r, raw, doc, log_rate, step_bias, skip_gain):
    lr, bias, skip = log_rate[None], step_bias[None], skip_gain[None]
    steps = raw.swapaxes(1, 2)
    hbm = pl.BlockSpec(memory_space=pltpu.HBM)
    send = call(
        outgoing_kernel,
        shape((STATE + 8, WIDTH)),
        scratch=(
            pltpu.VMEM((1, BLOCK), jnp.int32),
            pltpu.VMEM((1, HEADS, BLOCK), F32),
            pltpu.VMEM((1, HEADS), F32),
            pltpu.VMEM((1, HEADS), F32),
            pltpu.VMEM((BLOCK, WIDTH), BF16),
            pltpu.VMEM((BLOCK, STATE), BF16),
            pltpu.VMEM((STATE + 8, WIDTH), F32),
            pltpu.SemaphoreType.DMA((5 + PARTS,)),
            pltpu.SemaphoreType.DMA((PARTS + 1,)),
        ),
        flops=300_000_000,
        bytes_accessed=2 << 20,
        in_specs=[hbm] * 8,
        out_specs=hbm,
        limit=(64 << 10) - LEFT,
    )(doc, steps, bias, lr, x, c, w, r)
    got = lax.ppermute(send, "ctx", [(0, 1), (1, 0)])
    dxi, dp, heads, aux = call(
        intra_kernel,
        (shape((BLOCK, WIDTH)), shape((BLOCK, BLOCK)), shape((KEPT, BLOCK)), shape((EDGE + 8, BLOCK))),
        scratch=[pltpu.VMEM((BLOCK, BLOCK), F32)] * 2,
        flops=2_000_000_000,
        bytes_accessed=4 << 20,
    )(doc, steps, bias, lr, x, c, w, r)
    sums = call(
        sums_kernel,
        shape((1, 128)),
        flops=300_000_000,
        bytes_accessed=2 << 20,
    )(got, aux, x, c, w, r)
    total = mesh_sum(sums, lax.axis_size("dp"))
    grad_x, grad_w, grad_r, grad_step = call(
        grads_kernel,
        (
            shape((1, BLOCK, WIDTH), BF16),
            shape((1, BLOCK, STATE), BF16),
            shape((1, BLOCK, STATE), BF16),
            shape((1, HEADS, BLOCK)),
        ),
        flops=1_000_000_000,
        bytes_accessed=5 << 20,
    )(got, aux, heads, skip, x, c, w, r, dxi, dp)
    return (
        grad_x, grad_w, grad_r, grad_step.swapaxes(1, 2),
        total[0:HEADS], total[HEADS : 2 * HEADS], total[2 * HEADS : 3 * HEADS],
    )


def solution(mesh):
    split = P("dp", "ctx", None)
    return jax.shard_map(
        on_device,
        mesh=mesh,
        in_specs=(split, split, split, split, split, P("dp", "ctx"), P(), P(), P()),
        out_specs=(split, split, split, split, P(), P(), P()),
        check_vma=False,
    )
```

```python
import jax
import jax.numpy as jnp
from jax import lax
from jax.experimental import pallas as pl
from jax.experimental.pallas import tpu as pltpu
from jax.sharding import PartitionSpec as P

HEADS = 16
HEAD_DIM = 64
STATE = 256
BLOCK = 256
WIDTH = HEADS * HEAD_DIM
HALF = BLOCK // 2
PAIR = 2 * HEAD_DIM
F32 = jnp.float32
BF16 = jnp.bfloat16
NEG = -1e30
LOG2E = 1.4426950408889634

NN = (((1,), (0,)), ((), ()))
NT = (((1,), (1,)), ((), ()))


def dot(a, b, dims=NN):
    return lax.dot_general(a, b, dims, preferred_element_type=F32)


def split2(v):
    hi = v.astype(BF16)
    return hi, (v - hi.astype(F32)).astype(BF16)


def split3(v):
    hi = v.astype(BF16)
    rest = v - hi.astype(F32)
    mid = rest.astype(BF16)
    return hi, mid, (rest - mid.astype(F32)).astype(BF16)


def softplus(z):
    u = jnp.exp(-jnp.abs(z))
    series = u * (1.0 - u * (0.5 - u * (1.0 / 3.0 - u * 0.25)))
    return jnp.maximum(z, 0.0) + jnp.where(u < 0.01, series, jnp.log(1.0 + u))


def head_rows(count, start=0, width=WIDTH):
    lane = lax.broadcasted_iota(jnp.int32, (count, width), 1) + start
    row = lax.broadcasted_iota(jnp.int32, (count, width), 0)
    hit = lax.shift_right_logical(lane, 6) == (row & (HEADS - 1))
    return (hit & (row < 3 * HEADS)).astype(BF16)


def pieces(v):
    parts = [part.astype(F32) for part in split3(v)]
    rest = jnp.zeros((128 - 3 * HEADS, BLOCK), F32)
    return jnp.concatenate(parts + [rest], axis=0).T.astype(BF16)


def head_sums(v, rows):
    hi, lo = split2(v)
    return dot(rows, hi, NT) + dot(rows, lo, NT)


def triangle(upper):
    r = lax.broadcasted_iota(jnp.int32, (BLOCK, BLOCK), 0)
    c = lax.broadcasted_iota(jnp.int32, (BLOCK, BLOCK), 1)
    return ((r <= c) if upper else (r >= c)).astype(BF16)


def along_tokens(v, tri):
    count = v.shape[0]
    sums = dot(jnp.concatenate(split3(v), axis=0), tri)
    return sums[0:count] + sums[count : 2 * count] + sums[2 * count :]


def columns(row):
    return jnp.broadcast_to(row, (128, BLOCK)).T


def eye():
    r = lax.broadcasted_iota(jnp.int32, (HEADS, HEADS), 0)
    c = lax.broadcasted_iota(jnp.int32, (HEADS, HEADS), 1)
    return r == c


def to_column(row):
    return jnp.sum(jnp.where(eye(), row, 0.0), axis=1, keepdims=True)


def to_row(column):
    return jnp.sum(jnp.where(eye(), column, 0.0), axis=0, keepdims=True)


def head_arrays(raw, bias, lr):
    ell = jnp.exp(to_column(lr))
    z = raw + to_column(bias)
    s = softplus(z)
    return z, s, ell, s * -ell


def edge_gain(first, doc, s, cum):
    edge = jnp.where(first, doc[:, BLOCK - 1 :], doc[:, 0:1])
    arg = jnp.where(first, cum[:, BLOCK - 1 :] - cum, cum)
    gain = jnp.where(first, s, jnp.ones_like(s))
    return edge, jnp.where(doc == edge, jnp.exp(arg) * gain, 0.0)


PARTS = 4
PART = WIDTH // PARTS
STEP, GAIN, SIG, ELL, CUM, CUM_SIG, EDGE = (HEADS * n for n in range(7))
KEPT = EDGE + 8
COL, ROW = 0, HEADS
W_RATE, W_BIAS, OWN = 0, HEADS, 2 * HEADS


def outgoing_kernel(
    doc_hbm, raw_hbm, bias_hbm, lr_hbm, x_hbm, c_hbm, w_hbm, r_hbm,
    send_ref, heads_ref, x_ref, c_ref, w_ref, r_ref,
    doc_ref, raw_ref, bias_ref, lr_ref, sems,
):
    core = lax.axis_index("ctx")
    first = core == 0

    def fetch(src, dst, n):
        return pltpu.make_async_copy(src, dst, sems.at[n])

    small = [
        fetch(src, dst, n)
        for n, (src, dst) in enumerate(
            ((raw_hbm, raw_ref), (bias_hbm, bias_ref), (lr_hbm, lr_ref), (doc_hbm, doc_ref))
        )
    ]
    for copy in small:
        copy.start()

    def rows_of(src, dst, base):
        part = BLOCK // PARTS
        spans = [pl.ds(n * part, part) for n in range(PARTS)]
        return [fetch(src.at[:, span], dst.at[:, span], base + n) for n, span in enumerate(spans)]

    fetch_w, fetch_r = fetch(w_hbm, w_ref, 4), fetch(r_hbm, r_ref, 5)
    fetch_x, fetch_c = rows_of(x_hbm, x_ref, 6), rows_of(c_hbm, c_ref, 6 + PARTS)

    @pl.when(first)
    def _():
        for copy in [fetch_w] + fetch_x + [fetch_r] + fetch_c:
            copy.start()

    @pl.when(core == 1)
    def _():
        for copy in [fetch_r] + fetch_c + [fetch_w] + fetch_x:
            copy.start()

    tri = triangle(True)
    for copy in small:
        copy.wait()
    doc = doc_ref[...].astype(F32)
    z, s, ell, rate = head_arrays(raw_ref[0], bias_ref[...], lr_ref[...])
    sig = 1.0 / (1.0 + jnp.exp(-z))
    both = along_tokens(jnp.concatenate([rate, sig], axis=0), tri)
    edge, f = edge_gain(first, doc, s, both[0:HEADS])
    heads_ref[STEP:GAIN] = s
    heads_ref[GAIN:SIG] = f
    heads_ref[SIG:ELL] = sig
    heads_ref[ELL:CUM] = jnp.broadcast_to(ell, (HEADS, BLOCK))
    heads_ref[CUM:EDGE] = both
    heads_ref[EDGE:] = jnp.broadcast_to(edge, (8, BLOCK))
    send_ref[STATE:] = jnp.broadcast_to(edge, (8, WIDTH))
    by_token = pieces(f)

    def make_state(fetch_k, k_ref, fetch_v, v_ref):
        fetch_k.wait()
        k = k_ref[0].T
        for copy in fetch_v:
            copy.wait()
        for n in range(PARTS):
            lanes = slice(n * PART, (n + 1) * PART)
            wide = dot(by_token, head_rows(128, n * PART, PART))
            hi, lo = split2(v_ref[0, :, lanes].astype(F32) * wide)
            send_ref[0:STATE, lanes] = dot(k, hi) + dot(k, lo)

    @pl.when(first)
    def _():
        make_state(fetch_w, w_ref, fetch_x, x_ref)
        for copy in [fetch_r] + fetch_c:
            copy.wait()

    @pl.when(core == 1)
    def _():
        make_state(fetch_r, r_ref, fetch_c, c_ref)
        for copy in [fetch_w] + fetch_x:
            copy.wait()


def intra_kernel(
    doc_ref, heads_ref, x_ref, c_ref, w_ref, r_ref,
    dx_ref, dp_ref, stat_ref, aux_ref,
    mask_ref, p_ref,
):
    first = lax.axis_index("ctx") == 0
    doc = doc_ref[...].astype(F32)
    s, f, sig = heads_ref[STEP:GAIN], heads_ref[GAIN:SIG], heads_ref[SIG:ELL]
    ell, cum, cum_sig = heads_ref[ELL:CUM], heads_ref[CUM:CUM_SIG], heads_ref[CUM_SIG:EDGE]
    doc_col = columns(doc)
    for t in range(2):
        span = slice(t * HALF, (t + 1) * HALF)
        j = lax.broadcasted_iota(jnp.int32, (BLOCK, HALF), 0)
        i = lax.broadcasted_iota(jnp.int32, (BLOCK, HALF), 1) + t * HALF
        ok = (i >= j) & (doc_col == doc[:, span])
        mask_ref[:, span] = jnp.where(ok, 0.0, NEG)
    p_ref[...] = dot(w_ref[0], r_ref[0], NT)
    dp_ref[...] = jnp.zeros((BLOCK, BLOCK), F32)
    rows2 = cum * LOG2E
    cols2 = jnp.concatenate([(cum - jnp.log(s)) * LOG2E, jnp.zeros((128 - HEADS, BLOCK), F32)], axis=0).T
    lane = lax.broadcasted_iota(jnp.int32, (BLOCK, PAIR), 1)
    for pair in range(HEADS // 2):
        lanes = slice(pair * PAIR, (pair + 1) * PAIR)
        xp, cp = x_ref[0, :, lanes], c_ref[0, :, lanes]
        top = bottom = None
        for odd in range(2):
            h = 2 * pair + odd
            ch = jnp.where((lane < HEAD_DIM) != bool(odd), cp, jnp.zeros_like(cp))
            row = rows2[h : h + 1, :]
            col = cols2[:, h : h + 1]

            def tile(js, isl):
                g = dot(xp[js], ch[isl], NT)
                decay = jnp.exp2((row[:, isl] - col[js]) + mask_ref[js, isl])
                m = decay * p_ref[js, isl]
                dp_ref[js, isl] += decay * g
                hi, lo = split2(m)
                return dot(hi, ch[isl]) + dot(lo, ch[isl]), jnp.sum(m * g, axis=0, keepdims=True)

            d0, e0 = tile(slice(0, HALF), slice(0, BLOCK))
            d1, e1 = tile(slice(HALF, BLOCK), slice(HALF, BLOCK))
            stat_ref[ROW + h : ROW + h + 1, 0:HALF] = e0[:, 0:HALF]
            stat_ref[ROW + h : ROW + h + 1, HALF:] = e0[:, HALF:] + e1
            top = d0 if top is None else top + d0
            bottom = d1 if bottom is None else bottom + d1
        dx_ref[0:HALF, lanes] = top
        dx_ref[HALF:, lanes] = bottom
    rows = head_rows(HEADS)
    x = x_ref[0].astype(F32)
    q = head_sums(x * dx_ref[...], rows)
    stat_ref[COL:ROW] = q
    cx = jnp.sum(c_ref[0].astype(F32) * x, axis=0, keepdims=True)
    skip = sum(dot(rows, part, NT) for part in split3(jnp.broadcast_to(cx, (128, WIDTH))))
    da = stat_ref[ROW:] - q
    over = sig / s
    own_rate = jnp.sum(da * cum, axis=1, keepdims=True)
    own_bias = jnp.sum(q * over - ell * (da * cum_sig), axis=1, keepdims=True)
    own = [to_row(own_rate), to_row(own_bias), to_row(skip[:, 0:1])]
    own = jnp.concatenate(own + [jnp.zeros((1, BLOCK - 3 * HEADS), F32)], axis=1)
    w_rate = jnp.where(first, cum[:, BLOCK - 1 :] - cum, cum)
    w_bias = jnp.where(first, over + ell * (cum_sig - cum_sig[:, BLOCK - 1 :]), -ell * cum_sig)
    aux_ref[W_RATE:W_BIAS] = f * w_rate
    aux_ref[W_BIAS:OWN] = f * w_bias
    aux_ref[OWN:] = jnp.broadcast_to(own, (8, BLOCK))


def joined(got_ref, heads_ref):
    return (got_ref[STATE : STATE + 1, 0:1] == heads_ref[EDGE : EDGE + 1, 0:1]).astype(F32)


def sums_kernel(got_ref, heads_ref, aux_ref, x_ref, c_ref, w_ref, r_ref, sums_ref):
    first = lax.axis_index("ctx") == 0
    v = jnp.where(first, x_ref[0], c_ref[0]).astype(F32)
    k = jnp.where(first, w_ref[0], r_ref[0])
    t_hi, t_lo = split2(got_ref[0:STATE])
    z = dot(k, t_hi) + dot(k, t_lo)
    u = head_sums(v * z, head_rows(HEADS)) * joined(got_ref, heads_ref)
    sum_rate = to_row(jnp.sum(u * aux_ref[W_RATE:W_BIAS], axis=1, keepdims=True))
    sum_bias = to_row(jnp.sum(u * aux_ref[W_BIAS:OWN], axis=1, keepdims=True))
    rest = jnp.zeros((1, 128 - 2 * HEADS), F32)
    cross = jnp.concatenate([sum_rate, sum_bias, rest], axis=1)
    sums_ref[...] = aux_ref[OWN : OWN + 1, 0:128] + cross


def grads_kernel(
    got_ref, heads_ref, stat_ref, skip_ref, x_ref, c_ref, w_ref, r_ref, dxi_ref, dp_ref,
    dx_ref, dw_ref, dr_ref, dstep_ref,
):
    first = lax.axis_index("ctx") == 0
    f = heads_ref[GAIN:SIG] * joined(got_ref, heads_ref)
    wide = dot(pieces(f), head_rows(128))
    c = c_ref[0].astype(F32)
    v = jnp.where(first, x_ref[0], c_ref[0]).astype(F32)
    k = jnp.where(first, w_ref[0], r_ref[0])
    t_hi, t_lo = split2(got_ref[0:STATE])
    zs = (dot(k, t_hi) + dot(k, t_lo)) * wide
    hi, lo = split2(v * wide)
    dk = dot(hi, t_hi, NT) + dot(lo, t_hi, NT) + dot(hi, t_lo, NT)
    zero = jnp.zeros_like(dk)
    hi, lo = split2(dp_ref[...])
    dw = dot(hi, r_ref[0]) + dot(lo, r_ref[0])
    hi, lo = split2(dp_ref[...].T)
    dr = dot(hi, w_ref[0]) + dot(lo, w_ref[0])
    dw_ref[0] = (dw + jnp.where(first, dk, zero)).astype(BF16)
    dr_ref[0] = (dr + jnp.where(first, zero, dk)).astype(BF16)
    gains = dot(pieces(jnp.broadcast_to(to_column(skip_ref[...]), (HEADS, BLOCK))), head_rows(128))
    dx = dxi_ref[...] + jnp.where(first, zs, 0.0) + gains * c
    dx_ref[0] = dx.astype(BF16)
    u = head_sums(v * zs, head_rows(HEADS))
    q = stat_ref[COL:ROW] + jnp.where(first, u, 0.0)
    da = stat_ref[ROW:] - q + jnp.where(first, 0.0, u)
    drate = along_tokens(da, triangle(False))
    drate = drate + jnp.where(first, jnp.sum(u, axis=1, keepdims=True), 0.0)
    dstep = (q / heads_ref[STEP:GAIN] - drate * heads_ref[ELL:CUM]) * heads_ref[SIG:ELL]
    dstep_ref[0] = dstep


def call(kernel, outs, scratch=(), limit=40 << 10, flops=0, bytes_accessed=0, **specs):
    return pl.pallas_call(
        kernel,
        out_shape=outs,
        scratch_shapes=list(scratch),
        compiler_params=pltpu.CompilerParams(vmem_limit_bytes=limit << 10),
        cost_estimate=pl.CostEstimate(
            flops=flops, bytes_accessed=bytes_accessed, transcendentals=0
        ),
        **specs,
    )


def shape(dims, dtype=F32):
    return jax.ShapeDtypeStruct(dims, dtype)


def mesh_sum(sums, devices):
    both = lax.all_gather(sums, "ctx", axis=0, tiled=True)
    sums = both[0:1] + both[1:2]
    everyone = jnp.broadcast_to(sums, (devices, 128))
    everyone = lax.all_to_all(everyone, "dp", split_axis=0, concat_axis=0, tiled=True)
    return jnp.sum(everyone, axis=0)


def on_device(x, c, w, r, raw, doc, log_rate, step_bias, skip_gain):
    lr, bias, skip = log_rate[None], step_bias[None], skip_gain[None]
    steps = raw.swapaxes(1, 2)
    square, rows = shape((1, BLOCK, STATE), BF16), shape((1, BLOCK, WIDTH), BF16)
    inputs = [pltpu.with_memory_space_constraint(a, pltpu.HBM) for a in (doc, steps, bias, lr, x, c, w, r)]
    send, heads, x, c, w, r = call(
        outgoing_kernel,
        (shape((STATE + 8, WIDTH)), shape((KEPT, BLOCK)), rows, rows, square, square),
        scratch=(
            pltpu.VMEM((1, BLOCK), jnp.int32),
            pltpu.VMEM((1, HEADS, BLOCK), F32),
            pltpu.VMEM((1, HEADS), F32),
            pltpu.VMEM((1, HEADS), F32),
            pltpu.SemaphoreType.DMA((6 + 2 * PARTS,)),
        ),
        flops=300_000_000,
        bytes_accessed=2 << 20,
        in_specs=[pl.BlockSpec(memory_space=pltpu.HBM)] * 8,
    )(*inputs)
    got = lax.ppermute(send, "ctx", [(0, 1), (1, 0)])
    dxi, dp, stat, aux = call(
        intra_kernel,
        (shape((BLOCK, WIDTH)), shape((BLOCK, BLOCK)), shape((2 * HEADS, BLOCK)), shape((OWN + 8, BLOCK))),
        scratch=[pltpu.VMEM((BLOCK, BLOCK), F32)] * 2,
        flops=2_000_000_000,
        bytes_accessed=4 << 20,
    )(doc, heads, x, c, w, r)
    sums = call(
        sums_kernel,
        shape((1, 128)),
        flops=300_000_000,
        bytes_accessed=2 << 20,
    )(got, heads, aux, x, c, w, r)
    total = mesh_sum(sums, lax.axis_size("dp"))
    grad_x, grad_w, grad_r, grad_step = call(
        grads_kernel,
        (
            shape((1, BLOCK, WIDTH), BF16),
            shape((1, BLOCK, STATE), BF16),
            shape((1, BLOCK, STATE), BF16),
            shape((1, HEADS, BLOCK)),
        ),
        flops=1_000_000_000,
        bytes_accessed=5 << 20,
    )(got, heads, stat, skip, x, c, w, r, dxi, dp)
    return (
        grad_x, grad_w, grad_r, grad_step.swapaxes(1, 2),
        total[0:HEADS], total[HEADS : 2 * HEADS], total[2 * HEADS : 3 * HEADS],
    )


def solution(mesh):
    split = P("dp", "ctx", None)
    return jax.shard_map(
        on_device,
        mesh=mesh,
        in_specs=(split, split, split, split, split, P("dp", "ctx"), P(), P(), P()),
        out_specs=(split, split, split, split, P(), P(), P()),
        check_vma=False,
    )
```

```python
import jax
import jax.numpy as jnp
from jax import lax
from jax.experimental import pallas as pl
from jax.experimental.pallas import tpu as pltpu
from jax.sharding import PartitionSpec as P

HEADS = 16
HEAD_DIM = 64
STATE = 256
BLOCK = 256
WIDTH = HEADS * HEAD_DIM
HALF = BLOCK // 2
PAIR = 2 * HEAD_DIM
F32 = jnp.float32
BF16 = jnp.bfloat16
NEG = -1e30
LOG2E = 1.4426950408889634

NN = (((1,), (0,)), ((), ()))
NT = (((1,), (1,)), ((), ()))


def dot(a, b, dims=NN):
    return lax.dot_general(a, b, dims, preferred_element_type=F32)


def split2(v):
    hi = v.astype(BF16)
    return hi, (v - hi.astype(F32)).astype(BF16)


def split3(v):
    hi = v.astype(BF16)
    rest = v - hi.astype(F32)
    mid = rest.astype(BF16)
    return hi, mid, (rest - mid.astype(F32)).astype(BF16)


def softplus(z):
    u = jnp.exp(-jnp.abs(z))
    series = u * (1.0 - u * (0.5 - u * (1.0 / 3.0 - u * 0.25)))
    return jnp.maximum(z, 0.0) + jnp.where(u < 0.01, series, jnp.log(1.0 + u))


def head_rows(count, start=0, width=WIDTH):
    lane = lax.broadcasted_iota(jnp.int32, (count, width), 1) + start
    row = lax.broadcasted_iota(jnp.int32, (count, width), 0)
    hit = lax.shift_right_logical(lane, 6) == (row & (HEADS - 1))
    return (hit & (row < 3 * HEADS)).astype(BF16)


def pieces(v):
    parts = [part.astype(F32) for part in split3(v)]
    rest = jnp.zeros((128 - 3 * HEADS, BLOCK), F32)
    return jnp.concatenate(parts + [rest], axis=0).T.astype(BF16)


def head_sums(v, rows):
    hi, lo = split2(v)
    return dot(rows, hi, NT) + dot(rows, lo, NT)


def triangle(upper):
    r = lax.broadcasted_iota(jnp.int32, (BLOCK, BLOCK), 0)
    c = lax.broadcasted_iota(jnp.int32, (BLOCK, BLOCK), 1)
    return ((r <= c) if upper else (r >= c)).astype(BF16)


def along_tokens(v, tri):
    count = v.shape[0]
    sums = dot(jnp.concatenate(split3(v), axis=0), tri)
    return sums[0:count] + sums[count : 2 * count] + sums[2 * count :]


def columns(row):
    return jnp.broadcast_to(row, (128, BLOCK)).T


def eye():
    r = lax.broadcasted_iota(jnp.int32, (HEADS, HEADS), 0)
    c = lax.broadcasted_iota(jnp.int32, (HEADS, HEADS), 1)
    return r == c


def to_column(row):
    return jnp.sum(jnp.where(eye(), row, 0.0), axis=1, keepdims=True)


def to_row(column):
    return jnp.sum(jnp.where(eye(), column, 0.0), axis=0, keepdims=True)


def head_arrays(raw, bias, lr):
    ell = jnp.exp(to_column(lr))
    z = raw + to_column(bias)
    s = softplus(z)
    return z, s, ell, s * -ell


def edge_gain(first, doc, s, cum):
    edge = jnp.where(first, doc[:, BLOCK - 1 :], doc[:, 0:1])
    arg = jnp.where(first, cum[:, BLOCK - 1 :] - cum, cum)
    gain = jnp.where(first, s, jnp.ones_like(s))
    return edge, jnp.where(doc == edge, jnp.exp(arg) * gain, 0.0)


PARTS = 4
PART = WIDTH // PARTS
STEP, GAIN, SIG, ELL, CUM, CUM_SIG, EDGE = (HEADS * n for n in range(7))
KEPT = EDGE + 8
W_RATE, W_BIAS, OWN = 0, HEADS, 2 * HEADS
COL, ROW, PAIRS = OWN + 8, OWN + 8 + HEADS, OWN + 8 + 2 * HEADS


def outgoing_kernel(
    doc_hbm, raw_hbm, bias_hbm, lr_hbm, x_hbm, c_hbm, w_hbm, r_hbm,
    send_ref, heads_ref, x_ref, c_ref, w_ref, r_ref,
    doc_ref, raw_ref, bias_ref, lr_ref, sems,
):
    core = lax.axis_index("ctx")
    first = core == 0

    def fetch(src, dst, n):
        return pltpu.make_async_copy(src, dst, sems.at[n])

    small = [
        fetch(src, dst, n)
        for n, (src, dst) in enumerate(
            ((raw_hbm, raw_ref), (bias_hbm, bias_ref), (lr_hbm, lr_ref), (doc_hbm, doc_ref))
        )
    ]
    for copy in small:
        copy.start()

    def rows_of(src, dst, base):
        part = BLOCK // PARTS
        spans = [pl.ds(n * part, part) for n in range(PARTS)]
        return [fetch(src.at[:, span], dst.at[:, span], base + n) for n, span in enumerate(spans)]

    fetch_w, fetch_r = fetch(w_hbm, w_ref, 4), fetch(r_hbm, r_ref, 5)
    fetch_x, fetch_c = rows_of(x_hbm, x_ref, 6), rows_of(c_hbm, c_ref, 6 + PARTS)

    @pl.when(first)
    def _():
        for copy in [fetch_w] + fetch_x + [fetch_r] + fetch_c:
            copy.start()

    @pl.when(core == 1)
    def _():
        for copy in [fetch_r] + fetch_c + [fetch_w] + fetch_x:
            copy.start()

    tri = triangle(True)
    for copy in small:
        copy.wait()
    doc = doc_ref[...].astype(F32)
    z, s, ell, rate = head_arrays(raw_ref[0], bias_ref[...], lr_ref[...])
    sig = 1.0 / (1.0 + jnp.exp(-z))
    both = along_tokens(jnp.concatenate([rate, sig], axis=0), tri)
    edge, f = edge_gain(first, doc, s, both[0:HEADS])
    heads_ref[STEP:GAIN] = s
    heads_ref[GAIN:SIG] = f
    heads_ref[SIG:ELL] = sig
    heads_ref[ELL:CUM] = jnp.broadcast_to(ell, (HEADS, BLOCK))
    heads_ref[CUM:EDGE] = both
    heads_ref[EDGE:] = jnp.broadcast_to(edge, (8, BLOCK))
    send_ref[STATE:] = jnp.broadcast_to(edge, (8, WIDTH))
    by_token = pieces(f)

    def make_state(fetch_k, k_ref, fetch_v, v_ref):
        fetch_k.wait()
        k = k_ref[0].T
        for copy in fetch_v:
            copy.wait()
        for n in range(PARTS):
            lanes = slice(n * PART, (n + 1) * PART)
            wide = dot(by_token, head_rows(128, n * PART, PART))
            hi, lo = split2(v_ref[0, :, lanes].astype(F32) * wide)
            send_ref[0:STATE, lanes] = dot(k, hi) + dot(k, lo)

    @pl.when(first)
    def _():
        make_state(fetch_w, w_ref, fetch_x, x_ref)
        for copy in [fetch_r] + fetch_c:
            copy.wait()

    @pl.when(core == 1)
    def _():
        make_state(fetch_r, r_ref, fetch_c, c_ref)
        for copy in [fetch_w] + fetch_x:
            copy.wait()


def intra_kernel(
    doc_ref, heads_ref, x_ref, c_ref, w_ref, r_ref,
    dx_ref, aux_ref,
    mask_ref, p_ref,
):
    first = lax.axis_index("ctx") == 0
    doc = doc_ref[...].astype(F32)
    s, f, sig = heads_ref[STEP:GAIN], heads_ref[GAIN:SIG], heads_ref[SIG:ELL]
    ell, cum, cum_sig = heads_ref[ELL:CUM], heads_ref[CUM:CUM_SIG], heads_ref[CUM_SIG:EDGE]
    doc_col = columns(doc)
    for t in range(2):
        span = slice(t * HALF, (t + 1) * HALF)
        j = lax.broadcasted_iota(jnp.int32, (BLOCK, HALF), 0)
        i = lax.broadcasted_iota(jnp.int32, (BLOCK, HALF), 1) + t * HALF
        ok = (i >= j) & (doc_col == doc[:, span])
        mask_ref[:, span] = jnp.where(ok, 0.0, NEG)
    p_ref[...] = dot(w_ref[0], r_ref[0], NT)
    dp_ref = aux_ref.at[PAIRS:]
    dp_ref[...] = jnp.zeros((BLOCK, BLOCK), F32)
    rows2 = cum * LOG2E
    cols2 = jnp.concatenate([(cum - jnp.log(s)) * LOG2E, jnp.zeros((128 - HEADS, BLOCK), F32)], axis=0).T
    lane = lax.broadcasted_iota(jnp.int32, (BLOCK, PAIR), 1)
    for pair in range(HEADS // 2):
        lanes = slice(pair * PAIR, (pair + 1) * PAIR)
        xp, cp = x_ref[0, :, lanes], c_ref[0, :, lanes]
        top = bottom = None
        for odd in range(2):
            h = 2 * pair + odd
            ch = jnp.where((lane < HEAD_DIM) != bool(odd), cp, jnp.zeros_like(cp))
            row = rows2[h : h + 1, :]
            col = cols2[:, h : h + 1]

            def tile(js, isl):
                g = dot(xp[js], ch[isl], NT)
                decay = jnp.exp2((row[:, isl] - col[js]) + mask_ref[js, isl])
                m = decay * p_ref[js, isl]
                dp_ref[js, isl] += decay * g
                hi, lo = split2(m)
                return dot(hi, ch[isl]) + dot(lo, ch[isl]), jnp.sum(m * g, axis=0, keepdims=True)

            d0, e0 = tile(slice(0, HALF), slice(0, BLOCK))
            d1, e1 = tile(slice(HALF, BLOCK), slice(HALF, BLOCK))
            aux_ref[ROW + h : ROW + h + 1, 0:HALF] = e0[:, 0:HALF]
            aux_ref[ROW + h : ROW + h + 1, HALF:] = e0[:, HALF:] + e1
            top = d0 if top is None else top + d0
            bottom = d1 if bottom is None else bottom + d1
        dx_ref[0:HALF, lanes] = top
        dx_ref[HALF:, lanes] = bottom
    rows = head_rows(HEADS)
    x = x_ref[0].astype(F32)
    q = head_sums(x * dx_ref[...], rows)
    aux_ref[COL:ROW] = q
    cx = jnp.sum(c_ref[0].astype(F32) * x, axis=0, keepdims=True)
    skip = sum(dot(rows, part, NT) for part in split3(jnp.broadcast_to(cx, (128, WIDTH))))
    da = aux_ref[ROW:PAIRS] - q
    over = sig / s
    own_rate = jnp.sum(da * cum, axis=1, keepdims=True)
    own_bias = jnp.sum(q * over - ell * (da * cum_sig), axis=1, keepdims=True)
    own = [to_row(own_rate), to_row(own_bias), to_row(skip[:, 0:1])]
    own = jnp.concatenate(own + [jnp.zeros((1, BLOCK - 3 * HEADS), F32)], axis=1)
    w_rate = jnp.where(first, cum[:, BLOCK - 1 :] - cum, cum)
    w_bias = jnp.where(first, over + ell * (cum_sig - cum_sig[:, BLOCK - 1 :]), -ell * cum_sig)
    aux_ref[W_RATE:W_BIAS] = f * w_rate
    aux_ref[W_BIAS:OWN] = f * w_bias
    aux_ref[OWN:COL] = jnp.broadcast_to(own, (8, BLOCK))


def joined(got_ref, heads_ref):
    return (got_ref[STATE : STATE + 1, 0:1] == heads_ref[EDGE : EDGE + 1, 0:1]).astype(F32)


def sums_kernel(got_ref, heads_ref, aux_ref, x_ref, c_ref, w_ref, r_ref, sums_ref):
    first = lax.axis_index("ctx") == 0
    v = jnp.where(first, x_ref[0], c_ref[0]).astype(F32)
    k = jnp.where(first, w_ref[0], r_ref[0])
    t_hi, t_lo = split2(got_ref[0:STATE])
    z = dot(k, t_hi) + dot(k, t_lo)
    u = head_sums(v * z, head_rows(HEADS)) * joined(got_ref, heads_ref)
    sum_rate = to_row(jnp.sum(u * aux_ref[W_RATE:W_BIAS], axis=1, keepdims=True))
    sum_bias = to_row(jnp.sum(u * aux_ref[W_BIAS:OWN], axis=1, keepdims=True))
    rest = jnp.zeros((1, 128 - 2 * HEADS), F32)
    cross = jnp.concatenate([sum_rate, sum_bias, rest], axis=1)
    sums_ref[...] = aux_ref[OWN : OWN + 1, 0:128] + cross


def grads_kernel(
    got_ref, heads_ref, aux_ref, skip_ref, dxi_ref, x_hbm, c_hbm, w_hbm, r_hbm,
    dx_ref, dw_ref, dr_ref, dstep_ref,
    x_ref, c_ref, w_ref, r_ref, sems,
):
    pairs = ((w_hbm, w_ref), (r_hbm, r_ref), (x_hbm, x_ref), (c_hbm, c_ref))
    copies = [pltpu.make_async_copy(src, dst, sems.at[n]) for n, (src, dst) in enumerate(pairs)]
    for copy in copies:
        copy.start()
    first = lax.axis_index("ctx") == 0
    f = heads_ref[GAIN:SIG] * joined(got_ref, heads_ref)
    wide = dot(pieces(f), head_rows(128))
    gains = dot(pieces(jnp.broadcast_to(to_column(skip_ref[...]), (HEADS, BLOCK))), head_rows(128))
    t_hi, t_lo = split2(got_ref[0:STATE])
    for copy in copies[0:2]:
        copy.wait()
    k = jnp.where(first, w_ref[0], r_ref[0])
    zs = (dot(k, t_hi) + dot(k, t_lo)) * wide
    hi, lo = split2(aux_ref[PAIRS:])
    dw = dot(hi, r_ref[0]) + dot(lo, r_ref[0])
    hi, lo = split2(aux_ref[PAIRS:].T)
    dr = dot(hi, w_ref[0]) + dot(lo, w_ref[0])
    for copy in copies[2:]:
        copy.wait()
    c = c_ref[0].astype(F32)
    v = jnp.where(first, x_ref[0], c_ref[0]).astype(F32)
    hi, lo = split2(v * wide)
    dk = dot(hi, t_hi, NT) + dot(lo, t_hi, NT) + dot(hi, t_lo, NT)
    zero = jnp.zeros_like(dk)
    dw_ref[0] = (dw + jnp.where(first, dk, zero)).astype(BF16)
    dr_ref[0] = (dr + jnp.where(first, zero, dk)).astype(BF16)
    dx = dxi_ref[...] + jnp.where(first, zs, 0.0) + gains * c
    dx_ref[0] = dx.astype(BF16)
    u = head_sums(v * zs, head_rows(HEADS))
    q = aux_ref[COL:ROW] + jnp.where(first, u, 0.0)
    da = aux_ref[ROW:PAIRS] - q + jnp.where(first, 0.0, u)
    drate = along_tokens(da, triangle(False))
    drate = drate + jnp.where(first, jnp.sum(u, axis=1, keepdims=True), 0.0)
    dstep = (q / heads_ref[STEP:GAIN] - drate * heads_ref[ELL:CUM]) * heads_ref[SIG:ELL]
    dstep_ref[0] = dstep


def call(kernel, outs, scratch=(), limit=40 << 10, flops=0, bytes_accessed=0, **specs):
    return pl.pallas_call(
        kernel,
        out_shape=outs,
        scratch_shapes=list(scratch),
        compiler_params=pltpu.CompilerParams(vmem_limit_bytes=limit << 10),
        cost_estimate=pl.CostEstimate(
            flops=flops, bytes_accessed=bytes_accessed, transcendentals=0
        ),
        **specs,
    )


def shape(dims, dtype=F32):
    return jax.ShapeDtypeStruct(dims, dtype)


def mesh_sum(sums, devices):
    both = lax.all_gather(sums, "ctx", axis=0, tiled=True)
    sums = both[0:1] + both[1:2]
    everyone = jnp.broadcast_to(sums, (devices, 128))
    everyone = lax.all_to_all(everyone, "dp", split_axis=0, concat_axis=0, tiled=True)
    return jnp.sum(everyone, axis=0)


def on_device(x, c, w, r, raw, doc, log_rate, step_bias, skip_gain):
    lr, bias, skip = log_rate[None], step_bias[None], skip_gain[None]
    steps = raw.swapaxes(1, 2)
    square, rows = shape((1, BLOCK, STATE), BF16), shape((1, BLOCK, WIDTH), BF16)
    inputs = [pltpu.with_memory_space_constraint(a, pltpu.HBM) for a in (doc, steps, bias, lr, x, c, w, r)]
    send, heads, x, c, w, r = call(
        outgoing_kernel,
        (shape((STATE + 8, WIDTH)), shape((KEPT, BLOCK)), rows, rows, square, square),
        scratch=(
            pltpu.VMEM((1, BLOCK), jnp.int32),
            pltpu.VMEM((1, HEADS, BLOCK), F32),
            pltpu.VMEM((1, HEADS), F32),
            pltpu.VMEM((1, HEADS), F32),
            pltpu.SemaphoreType.DMA((6 + 2 * PARTS,)),
        ),
        flops=300_000_000,
        bytes_accessed=2 << 20,
        in_specs=[pl.BlockSpec(memory_space=pltpu.HBM)] * 8,
    )(*inputs)
    got = lax.ppermute(send, "ctx", [(0, 1), (1, 0)])
    dxi, aux = call(
        intra_kernel,
        (shape((BLOCK, WIDTH)), shape((PAIRS + BLOCK, BLOCK))),
        scratch=[pltpu.VMEM((BLOCK, BLOCK), F32)] * 2,
        flops=2_000_000_000,
        bytes_accessed=4 << 20,
    )(doc, heads, x, c, w, r)
    sums = call(
        sums_kernel,
        shape((1, 128)),
        flops=300_000_000,
        bytes_accessed=2 << 20,
    )(got, heads, aux, x, c, w, r)
    total = mesh_sum(sums, lax.axis_size("dp"))
    grad_x, grad_w, grad_r, grad_step = call(
        grads_kernel,
        (
            shape((1, BLOCK, WIDTH), BF16),
            shape((1, BLOCK, STATE), BF16),
            shape((1, BLOCK, STATE), BF16),
            shape((1, HEADS, BLOCK)),
        ),
        scratch=[pltpu.VMEM((1, BLOCK, WIDTH), BF16)] * 2
        + [pltpu.VMEM((1, BLOCK, STATE), BF16)] * 2
        + [pltpu.SemaphoreType.DMA((4,))],
        flops=1_000_000_000,
        bytes_accessed=5 << 20,
        in_specs=[pl.BlockSpec(memory_space=pltpu.VMEM)] * 5 + [pl.BlockSpec(memory_space=pltpu.HBM)] * 4,
    )(got, heads, aux, skip, dxi, *inputs[4:])
    return (
        grad_x, grad_w, grad_r, grad_step.swapaxes(1, 2),
        total[0:HEADS], total[HEADS : 2 * HEADS], total[2 * HEADS : 3 * HEADS],
    )


def solution(mesh):
    split = P("dp", "ctx", None)
    return jax.shard_map(
        on_device,
        mesh=mesh,
        in_specs=(split, split, split, split, split, P("dp", "ctx"), P(), P(), P()),
        out_specs=(split, split, split, split, P(), P(), P()),
        check_vma=False,
    )
```

```python
import jax
import jax.numpy as jnp
from jax import lax
from jax.experimental import pallas as pl
from jax.experimental.pallas import tpu as pltpu
from jax.sharding import PartitionSpec as P

HEADS = 16
HEAD_DIM = 64
STATE = 256
BLOCK = 256
WIDTH = HEADS * HEAD_DIM
HALF = BLOCK // 2
PAIR = 2 * HEAD_DIM
F32 = jnp.float32
BF16 = jnp.bfloat16
NEG = -1e30
LOG2E = 1.4426950408889634

NN = (((1,), (0,)), ((), ()))
NT = (((1,), (1,)), ((), ()))


def dot(a, b, dims=NN):
    return lax.dot_general(a, b, dims, preferred_element_type=F32)


def split2(v):
    hi = v.astype(BF16)
    return hi, (v - hi.astype(F32)).astype(BF16)


def split3(v):
    hi = v.astype(BF16)
    rest = v - hi.astype(F32)
    mid = rest.astype(BF16)
    return hi, mid, (rest - mid.astype(F32)).astype(BF16)


def softplus(z):
    u = jnp.exp(-jnp.abs(z))
    series = u * (1.0 - u * (0.5 - u * (1.0 / 3.0 - u * 0.25)))
    return jnp.maximum(z, 0.0) + jnp.where(u < 0.01, series, jnp.log(1.0 + u))


def head_rows(count, start=0, width=WIDTH):
    lane = lax.broadcasted_iota(jnp.int32, (count, width), 1) + start
    row = lax.broadcasted_iota(jnp.int32, (count, width), 0)
    hit = lax.shift_right_logical(lane, 6) == (row & (HEADS - 1))
    return (hit & (row < 3 * HEADS)).astype(BF16)


def pieces(v):
    parts = [part.astype(F32) for part in split3(v)]
    rest = jnp.zeros((128 - 3 * HEADS, BLOCK), F32)
    return jnp.concatenate(parts + [rest], axis=0).T.astype(BF16)


def head_sums(v, rows):
    hi, lo = split2(v)
    return dot(rows, hi, NT) + dot(rows, lo, NT)


def triangle(upper):
    r = lax.broadcasted_iota(jnp.int32, (BLOCK, BLOCK), 0)
    c = lax.broadcasted_iota(jnp.int32, (BLOCK, BLOCK), 1)
    return ((r <= c) if upper else (r >= c)).astype(BF16)


def along_tokens(v, tri):
    count = v.shape[0]
    sums = dot(jnp.concatenate(split3(v), axis=0), tri)
    return sums[0:count] + sums[count : 2 * count] + sums[2 * count :]


def columns(row):
    return jnp.broadcast_to(row, (128, BLOCK)).T


def eye():
    r = lax.broadcasted_iota(jnp.int32, (HEADS, HEADS), 0)
    c = lax.broadcasted_iota(jnp.int32, (HEADS, HEADS), 1)
    return r == c


def to_column(row):
    return jnp.sum(jnp.where(eye(), row, 0.0), axis=1, keepdims=True)


def to_row(column):
    return jnp.sum(jnp.where(eye(), column, 0.0), axis=0, keepdims=True)


def head_arrays(raw, bias, lr):
    ell = jnp.exp(to_column(lr))
    z = raw + to_column(bias)
    s = softplus(z)
    return z, s, ell, s * -ell


def edge_gain(first, doc, s, cum):
    edge = jnp.where(first, doc[:, BLOCK - 1 :], doc[:, 0:1])
    arg = jnp.where(first, cum[:, BLOCK - 1 :] - cum, cum)
    gain = jnp.where(first, s, jnp.ones_like(s))
    return edge, jnp.where(doc == edge, jnp.exp(arg) * gain, 0.0)


PARTS = 4
FETCHES = 1
PART = WIDTH // PARTS
STEP, GAIN, SIG, ELL, CUM, CUM_SIG, EDGE = (HEADS * n for n in range(7))
KEPT = EDGE + 8
W_RATE, W_BIAS, OWN = 0, HEADS, 2 * HEADS
COL, ROW, PAIRS = OWN + 8, OWN + 8 + HEADS, OWN + 8 + 2 * HEADS


def outgoing_kernel(
    doc_hbm, raw_hbm, bias_hbm, lr_hbm, x_hbm, c_hbm, w_hbm, r_hbm,
    send_ref, heads_ref, x_ref, c_ref, w_ref, r_ref,
    doc_ref, raw_ref, bias_ref, lr_ref, sems,
):
    core = lax.axis_index("ctx")
    first = core == 0

    def fetch(src, dst, n):
        return pltpu.make_async_copy(src, dst, sems.at[n])

    small = [
        fetch(src, dst, n)
        for n, (src, dst) in enumerate(
            ((raw_hbm, raw_ref), (bias_hbm, bias_ref), (lr_hbm, lr_ref), (doc_hbm, doc_ref))
        )
    ]
    for copy in small:
        copy.start()

    def rows_of(src, dst, base):
        part = BLOCK // FETCHES
        spans = [pl.ds(n * part, part) for n in range(FETCHES)]
        return [fetch(src.at[:, span], dst.at[:, span], base + n) for n, span in enumerate(spans)]

    fetch_w, fetch_r = fetch(w_hbm, w_ref, 4), fetch(r_hbm, r_ref, 5)
    fetch_x, fetch_c = rows_of(x_hbm, x_ref, 6), rows_of(c_hbm, c_ref, 6 + FETCHES)

    @pl.when(first)
    def _():
        for copy in [fetch_w] + fetch_x + [fetch_r] + fetch_c:
            copy.start()

    @pl.when(core == 1)
    def _():
        for copy in [fetch_r] + fetch_c + [fetch_w] + fetch_x:
            copy.start()

    tri = triangle(True)
    for copy in small:
        copy.wait()
    doc = doc_ref[...].astype(F32)
    z, s, ell, rate = head_arrays(raw_ref[0], bias_ref[...], lr_ref[...])
    sig = 1.0 / (1.0 + jnp.exp(-z))
    both = along_tokens(jnp.concatenate([rate, sig], axis=0), tri)
    edge, f = edge_gain(first, doc, s, both[0:HEADS])
    heads_ref[STEP:GAIN] = s
    heads_ref[GAIN:SIG] = f
    heads_ref[SIG:ELL] = sig
    heads_ref[ELL:CUM] = jnp.broadcast_to(ell, (HEADS, BLOCK))
    heads_ref[CUM:EDGE] = both
    heads_ref[EDGE:] = jnp.broadcast_to(edge, (8, BLOCK))
    send_ref[STATE:] = jnp.broadcast_to(edge, (8, WIDTH))
    by_token = pieces(f)

    def make_state(fetch_k, k_ref, fetch_v, v_ref):
        fetch_k.wait()
        k = k_ref[0].T
        for copy in fetch_v:
            copy.wait()
        for n in range(PARTS):
            lanes = slice(n * PART, (n + 1) * PART)
            wide = dot(by_token, head_rows(128, n * PART, PART))
            hi, lo = split2(v_ref[0, :, lanes].astype(F32) * wide)
            send_ref[0:STATE, lanes] = dot(k, hi) + dot(k, lo)

    @pl.when(first)
    def _():
        make_state(fetch_w, w_ref, fetch_x, x_ref)
        for copy in [fetch_r] + fetch_c:
            copy.wait()

    @pl.when(core == 1)
    def _():
        make_state(fetch_r, r_ref, fetch_c, c_ref)
        for copy in [fetch_w] + fetch_x:
            copy.wait()


def intra_kernel(
    doc_ref, heads_ref, x_ref, c_ref, w_ref, r_ref,
    dx_ref, aux_ref,
    mask_ref, p_ref,
):
    first = lax.axis_index("ctx") == 0
    doc = doc_ref[...].astype(F32)
    s, f, sig = heads_ref[STEP:GAIN], heads_ref[GAIN:SIG], heads_ref[SIG:ELL]
    ell, cum, cum_sig = heads_ref[ELL:CUM], heads_ref[CUM:CUM_SIG], heads_ref[CUM_SIG:EDGE]
    doc_col = columns(doc)
    for t in range(2):
        span = slice(t * HALF, (t + 1) * HALF)
        j = lax.broadcasted_iota(jnp.int32, (BLOCK, HALF), 0)
        i = lax.broadcasted_iota(jnp.int32, (BLOCK, HALF), 1) + t * HALF
        ok = (i >= j) & (doc_col == doc[:, span])
        mask_ref[:, span] = jnp.where(ok, 0.0, NEG)
    p_ref[...] = dot(w_ref[0], r_ref[0], NT)
    dp_ref = aux_ref.at[PAIRS:]
    dp_ref[...] = jnp.zeros((BLOCK, BLOCK), F32)
    rows2 = cum * LOG2E
    cols2 = jnp.concatenate([(cum - jnp.log(s)) * LOG2E, jnp.zeros((128 - HEADS, BLOCK), F32)], axis=0).T
    lane = lax.broadcasted_iota(jnp.int32, (BLOCK, PAIR), 1)
    for pair in range(HEADS // 2):
        lanes = slice(pair * PAIR, (pair + 1) * PAIR)
        xp, cp = x_ref[0, :, lanes], c_ref[0, :, lanes]
        top = None
        for odd in range(2):
            h = 2 * pair + odd
            ch = jnp.where((lane < HEAD_DIM) != bool(odd), cp, jnp.zeros_like(cp))
            row = rows2[h : h + 1, :]
            col = cols2[:, h : h + 1]

            g = dot(xp, ch, NT)

            def tile(js, isl):
                decay = jnp.exp2((row[:, isl] - col[js]) + mask_ref[js, isl])
                m = decay * p_ref[js, isl]
                dp_ref[js, isl] += decay * g[js, isl]
                return split2(m), jnp.sum(m * g[js, isl], axis=0, keepdims=True)

            (hi0, lo0), e0 = tile(slice(0, HALF), slice(0, BLOCK))
            (hi1, lo1), e1 = tile(slice(HALF, BLOCK), slice(HALF, BLOCK))
            zero = jnp.zeros_like(hi1)
            hi1, lo1 = (jnp.concatenate([zero, part], axis=1) for part in (hi1, lo1))
            d = dot(jnp.concatenate([hi0, hi1, lo0, lo1], axis=0), ch)
            d = d[0:BLOCK] + d[BLOCK:]
            aux_ref[ROW + h : ROW + h + 1, 0:HALF] = e0[:, 0:HALF]
            aux_ref[ROW + h : ROW + h + 1, HALF:] = e0[:, HALF:] + e1
            top = d if top is None else top + d
        dx_ref[:, lanes] = top
    rows = head_rows(HEADS)
    x = x_ref[0].astype(F32)
    q = head_sums(x * dx_ref[...], rows)
    aux_ref[COL:ROW] = q
    cx = jnp.sum(c_ref[0].astype(F32) * x, axis=0, keepdims=True)
    skip = sum(dot(rows, part, NT) for part in split3(jnp.broadcast_to(cx, (128, WIDTH))))
    da = aux_ref[ROW:PAIRS] - q
    over = sig / s
    own_rate = jnp.sum(da * cum, axis=1, keepdims=True)
    own_bias = jnp.sum(q * over - ell * (da * cum_sig), axis=1, keepdims=True)
    own = [to_row(own_rate), to_row(own_bias), to_row(skip[:, 0:1])]
    own = jnp.concatenate(own + [jnp.zeros((1, BLOCK - 3 * HEADS), F32)], axis=1)
    w_rate = jnp.where(first, cum[:, BLOCK - 1 :] - cum, cum)
    w_bias = jnp.where(first, over + ell * (cum_sig - cum_sig[:, BLOCK - 1 :]), -ell * cum_sig)
    aux_ref[W_RATE:W_BIAS] = f * w_rate
    aux_ref[W_BIAS:OWN] = f * w_bias
    aux_ref[OWN:COL] = jnp.broadcast_to(own, (8, BLOCK))


def joined(got_ref, heads_ref):
    return (got_ref[STATE : STATE + 1, 0:1] == heads_ref[EDGE : EDGE + 1, 0:1]).astype(F32)


def sums_kernel(got_ref, heads_ref, aux_ref, x_ref, c_ref, w_ref, r_ref, sums_ref):
    first = lax.axis_index("ctx") == 0
    v = jnp.where(first, x_ref[0], c_ref[0]).astype(F32)
    k = jnp.where(first, w_ref[0], r_ref[0])
    t_hi, t_lo = split2(got_ref[0:STATE])
    z = dot(k, t_hi) + dot(k, t_lo)
    u = head_sums(v * z, head_rows(HEADS)) * joined(got_ref, heads_ref)
    sum_rate = to_row(jnp.sum(u * aux_ref[W_RATE:W_BIAS], axis=1, keepdims=True))
    sum_bias = to_row(jnp.sum(u * aux_ref[W_BIAS:OWN], axis=1, keepdims=True))
    rest = jnp.zeros((1, 128 - 2 * HEADS), F32)
    cross = jnp.concatenate([sum_rate, sum_bias, rest], axis=1)
    sums_ref[...] = aux_ref[OWN : OWN + 1, 0:128] + cross


def grads_kernel(
    got_ref, heads_ref, aux_ref, skip_ref, dxi_ref, x_hbm, c_hbm, w_hbm, r_hbm,
    dx_ref, dw_ref, dr_ref, dstep_ref,
    x_ref, c_ref, w_ref, r_ref, sems,
):
    pairs = ((w_hbm, w_ref), (r_hbm, r_ref), (x_hbm, x_ref), (c_hbm, c_ref))
    copies = [pltpu.make_async_copy(src, dst, sems.at[n]) for n, (src, dst) in enumerate(pairs)]
    for copy in copies:
        copy.start()
    first = lax.axis_index("ctx") == 0
    f = heads_ref[GAIN:SIG] * joined(got_ref, heads_ref)
    wide = dot(pieces(f), head_rows(128))
    gains = dot(pieces(jnp.broadcast_to(to_column(skip_ref[...]), (HEADS, BLOCK))), head_rows(128))
    t_hi, t_lo = split2(got_ref[0:STATE])
    for copy in copies[0:2]:
        copy.wait()
    k = jnp.where(first, w_ref[0], r_ref[0])
    zs = (dot(k, t_hi) + dot(k, t_lo)) * wide
    hi, lo = split2(aux_ref[PAIRS:])
    dw = dot(hi, r_ref[0]) + dot(lo, r_ref[0])
    hi, lo = split2(aux_ref[PAIRS:].T)
    dr = dot(hi, w_ref[0]) + dot(lo, w_ref[0])
    for copy in copies[2:]:
        copy.wait()
    c = c_ref[0].astype(F32)
    v = jnp.where(first, x_ref[0], c_ref[0]).astype(F32)
    hi, lo = split2(v * wide)
    dk = dot(hi, t_hi, NT) + dot(lo, t_hi, NT) + dot(hi, t_lo, NT)
    zero = jnp.zeros_like(dk)
    dw_ref[0] = (dw + jnp.where(first, dk, zero)).astype(BF16)
    dr_ref[0] = (dr + jnp.where(first, zero, dk)).astype(BF16)
    dx = dxi_ref[...] + jnp.where(first, zs, 0.0) + gains * c
    dx_ref[0] = dx.astype(BF16)
    u = head_sums(v * zs, head_rows(HEADS))
    q = aux_ref[COL:ROW] + jnp.where(first, u, 0.0)
    da = aux_ref[ROW:PAIRS] - q + jnp.where(first, 0.0, u)
    drate = along_tokens(da, triangle(False))
    drate = drate + jnp.where(first, jnp.sum(u, axis=1, keepdims=True), 0.0)
    dstep = (q / heads_ref[STEP:GAIN] - drate * heads_ref[ELL:CUM]) * heads_ref[SIG:ELL]
    dstep_ref[0] = dstep


def call(kernel, outs, scratch=(), limit=40 << 10, flops=0, bytes_accessed=0, **specs):
    return pl.pallas_call(
        kernel,
        out_shape=outs,
        scratch_shapes=list(scratch),
        compiler_params=pltpu.CompilerParams(vmem_limit_bytes=limit << 10),
        cost_estimate=pl.CostEstimate(
            flops=flops, bytes_accessed=bytes_accessed, transcendentals=0
        ),
        **specs,
    )


def shape(dims, dtype=F32):
    return jax.ShapeDtypeStruct(dims, dtype)


def mesh_sum(sums, devices):
    both = lax.all_gather(sums, "ctx", axis=0, tiled=True)
    sums = both[0:1] + both[1:2]
    everyone = jnp.broadcast_to(sums, (devices, 128))
    everyone = lax.all_to_all(everyone, "dp", split_axis=0, concat_axis=0, tiled=True)
    return jnp.sum(everyone, axis=0)


def on_device(x, c, w, r, raw, doc, log_rate, step_bias, skip_gain):
    lr, bias, skip = log_rate[None], step_bias[None], skip_gain[None]
    steps = raw.swapaxes(1, 2)
    square, rows = shape((1, BLOCK, STATE), BF16), shape((1, BLOCK, WIDTH), BF16)
    inputs = [pltpu.with_memory_space_constraint(a, pltpu.HBM) for a in (doc, steps, bias, lr, x, c, w, r)]
    send, heads, x, c, w, r = call(
        outgoing_kernel,
        (shape((STATE + 8, WIDTH)), shape((KEPT, BLOCK)), rows, rows, square, square),
        scratch=(
            pltpu.VMEM((1, BLOCK), jnp.int32),
            pltpu.VMEM((1, HEADS, BLOCK), F32),
            pltpu.VMEM((1, HEADS), F32),
            pltpu.VMEM((1, HEADS), F32),
            pltpu.SemaphoreType.DMA((6 + 2 * FETCHES,)),
        ),
        flops=300_000_000,
        bytes_accessed=2 << 20,
        in_specs=[pl.BlockSpec(memory_space=pltpu.HBM)] * 8,
    )(*inputs)
    got = lax.ppermute(send, "ctx", [(0, 1), (1, 0)])
    dxi, aux = call(
        intra_kernel,
        (shape((BLOCK, WIDTH)), shape((PAIRS + BLOCK, BLOCK))),
        scratch=[pltpu.VMEM((BLOCK, BLOCK), F32)] * 2,
        flops=2_000_000_000,
        bytes_accessed=4 << 20,
    )(doc, heads, x, c, w, r)
    sums = call(
        sums_kernel,
        shape((1, 128)),
        flops=300_000_000,
        bytes_accessed=2 << 20,
    )(got, heads, aux, x, c, w, r)
    total = mesh_sum(sums, lax.axis_size("dp"))
    grad_x, grad_w, grad_r, grad_step = call(
        grads_kernel,
        (
            shape((1, BLOCK, WIDTH), BF16),
            shape((1, BLOCK, STATE), BF16),
            shape((1, BLOCK, STATE), BF16),
            shape((1, HEADS, BLOCK)),
        ),
        scratch=[pltpu.VMEM((1, BLOCK, WIDTH), BF16)] * 2
        + [pltpu.VMEM((1, BLOCK, STATE), BF16)] * 2
        + [pltpu.SemaphoreType.DMA((4,))],
        flops=1_000_000_000,
        bytes_accessed=5 << 20,
        in_specs=[pl.BlockSpec(memory_space=pltpu.VMEM)] * 5 + [pl.BlockSpec(memory_space=pltpu.HBM)] * 4,
    )(got, heads, aux, skip, dxi, *inputs[4:])
    return (
        grad_x, grad_w, grad_r, grad_step.swapaxes(1, 2),
        total[0:HEADS], total[HEADS : 2 * HEADS], total[2 * HEADS : 3 * HEADS],
    )


def solution(mesh):
    split = P("dp", "ctx", None)
    return jax.shard_map(
        on_device,
        mesh=mesh,
        in_specs=(split, split, split, split, split, P("dp", "ctx"), P(), P(), P()),
        out_specs=(split, split, split, split, P(), P(), P()),
        check_vma=False,
    )
```
